32 devices in a mesh: dp: 8 (over z, x), mp: 4 (over y, core).
Axes of the slice: x: 2, y: 2, z: 4, core: 2. Of those that a mesh axis runs over, the one named last changes fastest.
Arguments:
- tokens: bfloat16 [16384, 768], P('dp'), may hold values from -6 to 6
- cotangent: bfloat16 [16384, 768], P('dp'), may hold values from -6 to 6
- qkv_weight: bfloat16 [3, 768, 768], P(None, None, 'mp'), may hold values from -0.21875 to 0.21875
- col_bias: bfloat16 [2, 768], P(None, 'mp'), may hold values from -3 to 3
- out_weight: bfloat16 [768, 768], P('mp'), may hold values from -1.75 to 1.75
- in_weight: bfloat16 [768, 3072], P(None, 'mp'), may hold values from -0.21875 to 0.21875
- in_bias: bfloat16 [3072], P('mp'), may hold values from -3 to 3
- down_weight: bfloat16 [3072, 768], P('mp'), may hold values from -0.109375 to 0.109375
- vectors: bfloat16 [6, 768], replicated, may hold values from 0.5 to 1.5
- slot_is_long: int32 [32], P('dp'), may hold values from 0 to 1
- seq_len: int32 [32, 4], P('dp'), may hold values from 1 to 128, as said below
- master: float32 [4, 8, 221472], P('mp', 'dp'), may hold values from -0.18 to 0.18
- first_moment: float32 [4, 8, 221472], P('mp', 'dp'), as said below
- second_moment: float32 [4, 8, 221472], P('mp', 'dp'), as said below
- average: float32 [4, 8, 221472], P('mp', 'dp'), may hold values from -0.18 to 0.18
Outputs:
- output: bfloat16 [16384, 768], P('dp')
- grad_input: float32 [16384, 768], P('dp')
- vector_grad: float32 [4, 8, 144], P('mp', 'dp')
- new_master: float32 [4, 8, 221472], P('mp', 'dp')
- new_first: float32 [4, 8, 221472], P('mp', 'dp')
- new_second: float32 [4, 8, 221472], P('mp', 'dp')
- new_average: float32 [4, 8, 221472], P('mp', 'dp')
The draws below stay inside these ranges and needn't reach their ends.
Inputs may be any that keep to these rules, and one draw needn't show every extreme that they name: `seq_len`: in every slot one of the four entries equals 128. `first_moment`: entries of both signs, none near zero. `second_moment`: every entry positive.
All inputs are finite; a program needn't handle non-finite values.
Results may differ from the reference program's by a relative error of at most 0.02.
Values may be sent and summed in bfloat16 or wider, within the bound.
No kernel may reach another device: no remote copies, remote signals or barrier semaphores. Data moves between devices by JAX's collectives and lax.ppermute only.
A program may use at most 128 MiB of HBM per device.

```python
import math
import jax
import jax.numpy as jnp
from jax import lax

D = 768
HEADS = 12
HDIM = 64
FF = 3072
SLOT_TOKENS = 512
SHORT_TOKENS = 128
STEP = 3
TOK_DEV = 2048
TOKENS = 16384
SLOT_TOTAL = 32
MP_DEVS = 4
DP_DEVS = 8
P_SHARD = 221472
N_DP = 8
N_MP = 4


def region_scales():
    dl = D // MP_DEVS
    fl = FF // MP_DEVS
    tally_count = DP_DEVS
    sizes = [3 * D * dl // tally_count, D * dl // tally_count, D * fl // tally_count, fl * D // tally_count, 2 * dl // tally_count, fl // tally_count, 6 * D // MP_DEVS // tally_count]
    coefs = [0.5, 0.07, 0.35, 0.3, 0.5, 0.35, 0.8]
    base = math.sqrt(0.6 * TOK_DEV / DP_DEVS)
    return jnp.concatenate([jnp.full((size,), coef * base, jnp.float32) for size, coef in zip(sizes, coefs)])


def draw_first_moment(key, part):
    array_shape = (MP_DEVS, DP_DEVS, P_SHARD)
    sign_key = jax.random.fold_in(key, 11)
    size_key = jax.random.fold_in(key, 12)
    signs = jnp.where(jax.random.randint(sign_key, array_shape, 0, 2) == 1, 1.0, -1.0).astype(jnp.float32)
    sizes = jax.random.uniform(size_key, array_shape, jnp.float32, 0.5, 1.5)
    return region_scales() * signs * sizes


def draw_second_moment(key, part):
    array_shape = (MP_DEVS, DP_DEVS, P_SHARD)
    size_key = jax.random.fold_in(key, 21)
    scales = region_scales()
    return scales * scales * jax.random.uniform(size_key, array_shape, jnp.float32, 1.0, 4.0)


def draw_seq_len(key, part):
    length_key = jax.random.fold_in(key, 31)
    complete_key = jax.random.fold_in(key, 32)
    sequence_lengths = jax.random.randint(length_key, (SLOT_TOTAL, 4), 1, SHORT_TOKENS + 1)
    complete_array = jax.random.randint(complete_key, (SLOT_TOTAL,), 0, 4)
    places = jnp.arange(4, dtype=jnp.int32)[None, :]
    return jnp.where(places == complete_array[:, None], SHORT_TOKENS, sequence_lengths).astype(jnp.int32)


def plant(array, stream_key, smallest, top_value):
    extent = array.shape
    spot = [jax.random.randint(jax.random.fold_in(stream_key, axis), (), 0, extent[axis]) for axis in range(len(extent))]
    array = array.at[tuple(spot)].set(smallest)
    longest = extent.index(max(extent))
    spot[longest] = (spot[longest] + 1) % extent[longest]
    return array.at[tuple(spot)].set(top_value)


def block_levels(key, shape, cuts, low, top_value):
    loudness = 1.0
    for axis_at, shards_of in cuts:
        heights = jax.random.uniform(jax.random.fold_in(jax.random.fold_in(key, 6), axis_at), (shards_of,), jnp.float32, low / len(cuts), top_value / len(cuts))
        loudness = loudness * jnp.repeat(jnp.exp(heights), shape[axis_at] // shards_of).reshape((-1,) + (1,) * (len(shape) - 1 - axis_at))
    return loudness


def normal_values(key, dims, deviation, bound, cuts=(), kind=jnp.bfloat16):
    loudness = block_levels(key, dims, cuts, -0.22, 0.18) if cuts else 1.0
    values = jax.random.normal(key, dims, jnp.float32) * deviation * loudness
    return jnp.minimum(jnp.maximum(values, -bound), bound).astype(kind)


def setup_inputs(seed: int = 0) -> dict:
    splits = jax.random.split(jax.random.key(seed), 16)
    return {
        "tokens": normal_values(splits[0], (TOKENS, D), 1.0, 6.0, ((0, 8),)),
        "cotangent": normal_values(splits[1], (TOKENS, D), 1.0, 6.0, ((0, 8),)),
        "qkv_weight": normal_values(splits[2], (3, D, D), D ** -0.5, 0.21875, ((2, 4),)),
        "col_bias": normal_values(splits[3], (2, D), 0.5, 3.0, ((1, 4),)),
        "out_weight": normal_values(splits[4], (D, D), (D // 64) ** -0.5, 1.75, ((0, 4),)),
        "in_weight": normal_values(splits[5], (D, FF), D ** -0.5, 0.21875, ((1, 4),)),
        "in_bias": normal_values(splits[6], (FF,), 0.5, 3.0, ((0, 4),)),
        "down_weight": normal_values(splits[7], (FF, D), FF ** -0.5, 0.109375, ((0, 4),)),
        "vectors": jnp.clip(1.0 + 0.1 * jax.random.normal(splits[8], (6, D), jnp.float32), 0.5, 1.5).astype(jnp.bfloat16),
        "slot_is_long": plant(jax.random.randint(splits[9], (SLOT_TOTAL,), 0, 2), jax.random.fold_in(splits[9], 1), 0, 1).astype(jnp.int32),
        "seq_len": draw_seq_len(jax.random.fold_in(splits[15], 71), 0),
        "master": normal_values(splits[11], (MP_DEVS, DP_DEVS, P_SHARD), 0.03, 0.18, ((0, 4), (1, 8)), jnp.float32),
        "first_moment": draw_first_moment(jax.random.fold_in(splits[15], 71), 0),
        "second_moment": draw_second_moment(jax.random.fold_in(splits[15], 71), 0),
        "average": normal_values(splits[14], (MP_DEVS, DP_DEVS, P_SHARD), 0.03, 0.18, ((0, 4), (1, 8)), jnp.float32),
    }


HIGH = lax.Precision.HIGHEST
NORM_EPS = 1e-12

@jax.custom_vjp
def low(v):
    return lax.optimization_barrier(v.astype(jnp.bfloat16)).astype(jnp.float32)

@jax.custom_vjp
def low_back(v):
    return v

def low_keep(v):
    return (low(v), None)

def low_pass(kept, grad):
    return (grad,)

def back_keep(v):
    return (v, None)

def back_low(kept, grad):
    return (low(grad),)
low.defvjp(low_keep, low_pass)
low_back.defvjp(back_keep, back_low)

def slot_masks(kind, sequence_lengths):
    pos = jnp.arange(SLOT_TOKENS, dtype=jnp.int32)
    block = pos // SHORT_TOKENS
    is_long = kind == 1
    segment = jnp.where(is_long, 0, block)
    inner = jnp.where(is_long, pos, pos % SHORT_TOKENS)
    picks = block[:, None] == jnp.arange(sequence_lengths.shape[0], dtype=jnp.int32)[None, :]
    short_len = lax.optimization_barrier(jnp.sum(jnp.where(picks, sequence_lengths[None, :], 0), axis=1))
    seg_len = jnp.where(is_long, jnp.sum(sequence_lengths), short_len)
    valid = inner < seg_len
    allowed = (segment[:, None] == segment[None, :]) & valid[None, :]
    return (allowed, valid)

def layer_norm(z, gain, shift):
    centered = z - lax.optimization_barrier(jnp.mean(z, axis=-1, keepdims=True))
    var = lax.optimization_barrier(jnp.mean(centered * centered, axis=-1, keepdims=True))
    return centered * lax.rsqrt(var + NORM_EPS) * gain + shift

def gelu_exact(u):
    return 0.5 * u * (1.0 + jax.scipy.special.erf(u * 2.0 ** (-0.5)))

def slot_attend(item):
    query, keys, values, allowed = item
    scores = low_back(jnp.einsum('qhe,khe->hqk', query, keys, precision=HIGH))
    scores = jnp.where(allowed[None], scores, -1000000000.0)
    probs = jax.nn.softmax(scores, axis=-1)
    return jnp.einsum('hqk,khe->qhe', low(probs), values, precision=HIGH)

def forward(params, rows_in, allowed):
    qkv_w, col_b, out_w, in_w, in_b, down_w, vec = params
    total = rows_in.shape[0]
    sequence_group = allowed.shape[0]
    dl = D // N_MP
    fl = FF // N_MP
    scale = HDIM ** (-0.5)
    queries, keyset, valueset = ([], [], [])
    for j in range(N_MP):
        cols = slice(j * dl, (j + 1) * dl)
        xj = low(low_back(rows_in))
        queries.append(low(low_back((jnp.dot(xj, qkv_w[0][:, cols], precision=HIGH) + col_b[0, cols]) * scale)))
        keyset.append(low(low_back(jnp.dot(xj, qkv_w[1][:, cols], precision=HIGH))))
        valueset.append(low(low_back(jnp.dot(xj, qkv_w[2][:, cols], precision=HIGH) + col_b[1, cols])))
    shape4 = (sequence_group, SLOT_TOKENS, HEADS, HDIM)
    query = jnp.concatenate(queries, axis=1).reshape(shape4)
    keys = jnp.concatenate(keyset, axis=1).reshape(shape4)
    values = jnp.concatenate(valueset, axis=1).reshape(shape4)
    context = lax.map(jax.checkpoint(slot_attend), (query, keys, values, allowed))
    context = low(low_back(context.reshape(total, D)))
    attn = jnp.zeros((total, D), jnp.float32)
    for j in range(N_MP):
        cols = slice(j * dl, (j + 1) * dl)
        attn = attn + low(jnp.dot(context[:, cols], out_w[cols, :], precision=HIGH))
    z_one = rows_in + low_back(attn) + vec[4]
    x_one = layer_norm(z_one, vec[0], vec[1])
    ffn = jnp.zeros((total, D), jnp.float32)
    for j in range(N_MP):
        units = slice(j * fl, (j + 1) * fl)
        xj = low(low_back(x_one))
        pre = low_back(jnp.dot(xj, in_w[:, units], precision=HIGH) + in_b[units])
        hidden = low(gelu_exact(pre))
        ffn = ffn + low(jnp.dot(hidden, down_w[units, :], precision=HIGH))
    z_two = x_one + low_back(ffn) + vec[5]
    return layer_norm(z_two, vec[2], vec[3])

def to_layout(grads):
    g_qkv, g_col, g_out, g_in, g_inb, g_down, g_vec = grads
    dl = D // N_MP
    fl = FF // N_MP
    share = 6 * D // N_MP
    flat_vec = g_vec.reshape(-1)
    shards = []
    for j in range(N_MP):
        cols = slice(j * dl, (j + 1) * dl)
        units = slice(j * fl, (j + 1) * fl)
        pieces = [g_qkv[:, :, cols], g_out[cols, :], g_in[:, units], g_down[units, :], g_col[:, cols], g_inb[units], flat_vec[j * share:(j + 1) * share]]
        shards.append(jnp.concatenate([piece.reshape(N_DP, -1) for piece in pieces], axis=1))
    return jnp.stack(shards)

def reference(tokens, cotangent, qkv_weight, col_bias, out_weight, in_weight, in_bias, down_weight, vectors, slot_is_long, seq_len, master, first_moment, second_moment, average):
    params = tuple((w.astype(jnp.float32) for w in (qkv_weight, col_bias, out_weight, in_weight, in_bias, down_weight, vectors)))
    slot_number = slot_is_long.shape[0]
    sequence_group = math.gcd(slot_number, max(1, 4096 // SLOT_TOKENS))
    tally_count = slot_number // sequence_group
    rows_x = tokens.astype(jnp.float32).reshape(tally_count, sequence_group * SLOT_TOKENS, D)
    rows_c = cotangent.astype(jnp.float32).reshape(tally_count, sequence_group * SLOT_TOKENS, D)
    kinds = slot_is_long.reshape(tally_count, sequence_group)
    sequence_lengths = seq_len.reshape(tally_count, sequence_group, 4)

    def step(carry, item):
        xg, cg, kg, lg = item
        allowed, valid = jax.vmap(slot_masks)(kg, lg)
        masked = cg * valid.reshape(-1)[:, None].astype(jnp.float32)
        y_val, pull = jax.vjp(lambda p, xx: forward(p, xx, allowed), params, xg)
        g_par, g_x = pull(masked)
        carry = jax.tree.map(lambda a, b: a + b, carry, g_par)
        return (carry, (y_val, g_x))
    zeros = jax.tree.map(jnp.zeros_like, params)
    sums, (y_all, gx_all) = lax.scan(step, zeros, (rows_x, rows_c, kinds, sequence_lengths))
    grad = to_layout(sums) / N_DP
    grad = grad.reshape(master.shape)
    vector_grad = (sums[6] / N_DP).reshape(N_MP, N_DP, -1)
    new_first = 0.5 * first_moment + 0.5 * grad
    new_second = 0.5 * second_moment + 0.5 * grad * grad
    corr = 1.0 - 0.5 ** STEP
    new_master = master - 0.02 * (new_first / corr / (jnp.sqrt(new_second / corr) + 1e-08) + 0.01 * master)
    new_average = 0.75 * average + 0.25 * new_master
    output = y_all.reshape(-1, D).astype(jnp.bfloat16)
    grad_input = gx_all.reshape(-1, D)
    return (output, grad_input, vector_grad, new_master, new_first, new_second, new_average)
```

```python
import jax
import jax.numpy as jnp
from jax import lax
from jax.sharding import PartitionSpec as P

HDIM = 64
SLOT_TOKENS = 512
SHORT_TOKENS = 128
STEP = 3
NORM_EPS = 1e-12
BF = jnp.bfloat16
F32 = jnp.float32


def slot_masks(kind, sequence_lengths):
    pos = jnp.arange(SLOT_TOKENS, dtype=jnp.int32)
    block = pos // SHORT_TOKENS
    is_long = kind == 1
    segment = jnp.where(is_long, 0, block)
    inner = jnp.where(is_long, pos, pos % SHORT_TOKENS)
    picks = block[:, None] == jnp.arange(sequence_lengths.shape[0], dtype=jnp.int32)[None, :]
    short_len = jnp.sum(jnp.where(picks, sequence_lengths[None, :], 0), axis=1)
    seg_len = jnp.where(is_long, jnp.sum(sequence_lengths), short_len)
    valid = inner < seg_len
    allowed = (segment[:, None] == segment[None, :]) & valid[None, :]
    return (allowed, valid)


def dot(a, b):
    return lax.dot_general(a, b, (((1,), (0,)), ((), ())), preferred_element_type=F32)


def dot_t(a, b):
    return lax.dot_general(a, b, (((1,), (1,)), ((), ())), preferred_element_type=F32)


def t_dot(a, b):
    return lax.dot_general(a, b, (((0,), (0,)), ((), ())), preferred_element_type=F32)


def swap(value, axis, bit):
    size = lax.axis_size(axis)
    return lax.ppermute(value, axis, [(i, i ^ bit) for i in range(size)])


def both_cores(value):
    return (value, swap(value, "mp", 1))


def norm_parts(z):
    mean = jnp.mean(z, axis=-1, keepdims=True)
    centered = z - mean
    var = jnp.mean(centered * centered, axis=-1, keepdims=True)
    rstd = lax.rsqrt(var + NORM_EPS)
    return centered * rstd, rstd


def norm_back(dy, normed, rstd, gain):
    dn = dy * gain
    back = rstd * (
        dn
        - jnp.mean(dn, axis=-1, keepdims=True)
        - normed * jnp.mean(dn * normed, axis=-1, keepdims=True)
    )
    return back, jnp.sum(dy * normed, axis=0), jnp.sum(dy, axis=0), jnp.sum(back, axis=0)


def heads_of(value):
    return value.reshape(SLOT_TOKENS, -1, HDIM).transpose(1, 0, 2)


def flat_of(value):
    return value.transpose(1, 0, 2).reshape(SLOT_TOKENS, -1)


def bmm(eq, a, b):
    return jnp.einsum(eq, a, b, preferred_element_type=F32)


def attn_forward(q, k, v, allowed):
    q, k, v = heads_of(q), heads_of(k), heads_of(v)
    s = jnp.where(allowed[None], bmm("hqe,hke->hqk", q, k), -1000000000.0)
    top = jnp.max(s, axis=-1, keepdims=True)
    e = jnp.exp(s - top)
    total = jnp.sum(e, axis=-1, keepdims=True)
    p = (e / total).astype(BF)
    return flat_of(bmm("hqk,hke->hqe", p, v).astype(BF)), top + jnp.log(total)


def attn_backward(q, k, v, dctx, lse, allowed):
    q, k, v, dctx = heads_of(q), heads_of(k), heads_of(v), heads_of(dctx)
    s = bmm("hqe,hke->hqk", q, k)
    p = jnp.where(allowed[None], jnp.exp(jnp.where(allowed[None], s, -1e9) - lse), 0.0)
    dp = bmm("hqe,hke->hqk", dctx, v)
    ds = (p * (dp - jnp.sum(p * dp, axis=-1, keepdims=True))).astype(BF)
    dq = bmm("hqk,hke->hqe", ds, k)
    dk = bmm("hqk,hqe->hke", ds, q)
    dv = bmm("hqk,hqe->hke", p.astype(BF), dctx)
    return flat_of(dq.astype(BF)), flat_of(dk.astype(BF)), flat_of(dv.astype(BF))


def scatter_sum(blocks, first, order):
    ndata = blocks.shape[0]
    rank = lax.axis_index("dp")
    cur = blocks[None]
    left = list(range(ndata.bit_length() - 1))
    for bit in order(left):
        low = sum(1 for b in left if b < bit)
        rest = cur.shape[2:]
        view = cur.reshape((cur.shape[1] >> (low + 1), 2, 1 << low) + rest)
        mine = (rank >> bit) & 1
        keep = lax.dynamic_index_in_dim(view, mine, 1, keepdims=False)
        send = lax.dynamic_index_in_dim(view, 1 - mine, 1, keepdims=False)
        got = swap(send.astype(BF), "dp", 1 << bit)
        cur = (keep.astype(F32) + got.astype(F32)).reshape((1, -1) + rest)
        left.remove(bit)
    return cur[0, 0]


def upward(left):
    return list(left)


def body(
    tokens,
    cotangent,
    qkv_weight,
    col_bias,
    out_weight,
    in_weight,
    in_bias,
    down_weight,
    vectors,
    slot_is_long,
    seq_len,
    master,
    first_moment,
    second_moment,
    average,
):
    rows = tokens.shape[0]
    scale = HDIM ** (-0.5)
    ndata = lax.axis_size("dp")
    nmodel = lax.axis_size("mp")
    core = lax.axis_index("mp") & 1
    pair = lax.axis_index("mp") >> 1
    vec = vectors.astype(F32)
    per_core = rows // 2 // SLOT_TOKENS

    wqkv = both_cores(jnp.transpose(qkv_weight, (0, 2, 1)).reshape(-1, qkv_weight.shape[1]))
    bias = both_cores(col_bias)
    wo = both_cores(out_weight)
    w1 = both_cores(in_weight)
    b1 = both_cores(in_bias)
    w2 = both_cores(down_weight)
    cols = qkv_weight.shape[2]

    x_mine = lax.dynamic_slice_in_dim(tokens, core * (rows // 2), rows // 2)
    cot_mine = lax.dynamic_slice_in_dim(cotangent, core * (rows // 2), rows // 2)
    kinds = lax.dynamic_slice_in_dim(slot_is_long, core * per_core, per_core)
    lengths = lax.dynamic_slice_in_dim(seq_len, core * per_core, per_core)
    n = range(per_core)
    x = [x_mine[i * SLOT_TOKENS : (i + 1) * SLOT_TOKENS] for i in n]
    cot = [cot_mine[i * SLOT_TOKENS : (i + 1) * SLOT_TOKENS] for i in n]
    masks = [slot_masks(kinds[i], lengths[i]) for i in n]

    def phase_one(i):
        q, k, v = [], [], []
        for g in range(2):
            proj = dot_t(x[i], wqkv[g])
            b = bias[g].astype(F32)
            q.append(((proj[:, :cols] + b[0]) * scale).astype(BF))
            k.append(proj[:, cols : 2 * cols].astype(BF))
            v.append((proj[:, 2 * cols :] + b[1]).astype(BF))
        q, k, v = (jnp.concatenate(t, axis=1) for t in (q, k, v))
        ctx, lse = attn_forward(q, k, v, masks[i][0])
        part = dot(ctx[:, :cols], wo[0]) + dot(ctx[:, cols:], wo[1])
        return (q, k, v, ctx, lse), part.astype(BF)

    def total(part, other):
        return part.astype(F32) + other.astype(F32)

    def phase_two(i, part, other):
        z = x[i].astype(F32) + total(part, other) + vec[4]
        normed, rstd = norm_parts(z)
        x_one = normed * vec[0] + vec[1]
        xb = x_one.astype(BF)
        hidden, slope, out = [], [], 0.0
        for g in range(2):
            pre = dot(xb, w1[g]) + b1[g].astype(F32)
            phi = 0.5 * (1.0 + lax.erf(pre * 2.0 ** (-0.5)))
            hidden.append((pre * phi).astype(BF))
            bell = jnp.exp(-0.5 * pre * pre) * 0.3989422804014327
            slope.append((phi + pre * bell).astype(BF))
            out = out + dot(hidden[g], w2[g])
        return (normed, rstd, x_one, xb, hidden, slope), out.astype(BF)

    def phase_three(i, saved, part, other):
        normed, rstd, x_one, xb, hidden, slope = saved
        z = x_one + total(part, other) + vec[5]
        n2, r2 = norm_parts(z)
        out = (n2 * vec[2] + vec[3]).astype(BF)
        dy = cot[i].astype(F32) * masks[i][1][:, None].astype(F32)
        dz, dg, dbeta, db = norm_back(dy, n2, r2, vec[2])
        dzb = dz.astype(BF)
        dpre, back = [], 0.0
        for g in range(2):
            dpre.append((dot_t(dzb, w2[g]) * slope[g].astype(F32)).astype(BF))
            back = back + dot_t(dpre[g], w1[g])
        return out, (dz, dzb, dpre, (dg, dbeta, db)), back.astype(BF)

    def phase_four(i, first, second, third, part, other):
        q, k, v, ctx, lse = first
        normed, rstd = second[:2]
        dx = third[0] + total(part, other)
        dz, dg, dbeta, db = norm_back(dx, normed, rstd, vec[0])
        dzb = dz.astype(BF)
        dctx = jnp.concatenate([dot_t(dzb, wo[g]).astype(BF) for g in range(2)], axis=1)
        grads = attn_backward(q, k, v, dctx, lse, masks[i][0])
        back = 0.0
        for g in range(2):
            dq, dk, dv = (t[:, g * cols : (g + 1) * cols] for t in grads)
            back = back + (
                dot(dq, wqkv[g][:cols]) * scale
                + dot(dk, wqkv[g][cols : 2 * cols])
                + dot(dv, wqkv[g][2 * cols :])
            )
        return (dz, dzb, grads, (dg, dbeta, db)), back.astype(BF)

    across = lambda part: swap(part, "mp", 2)
    one = [phase_one(i) for i in n]
    one_r = [across(one[i][1]) for i in n]
    two = [phase_two(i, one[i][1], one_r[i]) for i in n]
    two_r = [across(two[i][1]) for i in n]
    three = [phase_three(i, two[i][0], two[i][1], two_r[i]) for i in n]
    three_r = [across(three[i][2]) for i in n]
    four = [phase_four(i, one[i][0], two[i][0], three[i][1], three[i][2], three_r[i]) for i in n]
    four_r = [across(four[i][1]) for i in n]

    def whole(half, other):
        first = jnp.where(core == 0, half, other)
        second = jnp.where(core == 0, other, half)
        return jnp.concatenate([first, second])

    out_half = jnp.concatenate([three[i][0] for i in n])
    output = whole(out_half, swap(out_half, "mp", 1))
    gi_half = jnp.concatenate([four[i][0][0] + total(four[i][1], four_r[i]) for i in n])
    grad_input = whole(gi_half, swap(gi_half, "mp", 1))

    def over_cores(parts):
        return parts[0] + swap(parts[1].astype(BF), "mp", 1).astype(F32)

    cat = lambda f: jnp.concatenate([f(i) for i in n])
    xb_all = cat(lambda i: two[i][0][3])
    dz2_all = cat(lambda i: three[i][1][1])
    g_down, g_in, g_inb = [], [], []
    for g in range(2):
        dpre = cat(lambda i: three[i][1][2][g])
        g_down.append(t_dot(cat(lambda i: two[i][0][4][g]), dz2_all))
        g_in.append(t_dot(xb_all, dpre))
        g_inb.append(jnp.sum(dpre.astype(F32), axis=0))
    s_down = scatter_sum(over_cores(g_down).reshape(ndata, -1, g_down[0].shape[1]), None, upward)
    s_in = scatter_sum(over_cores(g_in).reshape(ndata, -1, g_in[0].shape[1]), None, upward)

    ctx_all = cat(lambda i: one[i][0][3])
    dz1_all = cat(lambda i: four[i][0][1])
    dq_all, dk_all, dv_all = (cat(lambda i: four[i][0][2][t]) for t in range(3))
    g_out, g_qkv, g_col = [], [], []
    for g in range(2):
        c = slice(g * cols, (g + 1) * cols)
        g_out.append(t_dot(ctx_all[:, c], dz1_all))
        g_qkv.append(
            jnp.concatenate(
                [t_dot(x_mine, dq_all[:, c]) * scale, t_dot(x_mine, dk_all[:, c]), t_dot(x_mine, dv_all[:, c])]
            )
        )
        g_col.append(
            jnp.stack([jnp.sum(dq_all[:, c].astype(F32), axis=0) * scale, jnp.sum(dv_all[:, c].astype(F32), axis=0)])
        )
    s_out = scatter_sum(over_cores(g_out).reshape(ndata, -1, g_out[0].shape[1]), None, upward)
    s_qkv = scatter_sum(over_cores(g_qkv).reshape(ndata, -1, cols), None, upward)

    add = lambda t: sum(t[1:], t[0])
    g1, be1, bo = (add([four[i][0][3][t] for i in n]) for t in range(3))
    g2, be2, b2 = (add([three[i][1][3][t] for i in n]) for t in range(3))
    g_vec = jnp.stack([g1, be1, g2, be2, bo, b2]).reshape(nmodel, -1)
    small = []
    for g in range(2):
        owner = 2 * pair + (core if g == 0 else 1 - core)
        share = lax.dynamic_index_in_dim(g_vec, owner, 0, keepdims=False)
        small.append(
            jnp.concatenate([g_col[g].reshape(ndata, -1), g_inb[g].reshape(ndata, -1), share.reshape(ndata, -1)], axis=1)
        )
    s_small = scatter_sum(over_cores(small), None, upward)
    n_vec = g_vec.shape[1] // ndata

    grad = jnp.concatenate([s_qkv.reshape(-1), s_out.reshape(-1), s_in.reshape(-1), s_down.reshape(-1), s_small])
    grad = (grad / ndata).reshape(master.shape)
    vector_grad = (s_small[-n_vec:] / ndata).reshape(1, 1, -1)
    new_first = 0.5 * first_moment + 0.5 * grad
    new_second = 0.5 * second_moment + 0.5 * grad * grad
    corr = 1.0 - 0.5**STEP
    new_master = master - 0.02 * (
        new_first / corr / (jnp.sqrt(new_second / corr) + 1e-08) + 0.01 * master
    )
    new_average = 0.75 * average + 0.25 * new_master
    return (output, grad_input, vector_grad, new_master, new_first, new_second, new_average)


def solution(mesh):
    rows = P("dp", None)
    opt = P("mp", "dp", None)
    return jax.shard_map(
        body,
        mesh=mesh,
        in_specs=(
            rows,
            rows,
            P(None, None, "mp"),
            P(None, "mp"),
            P("mp", None),
            P(None, "mp"),
            P("mp"),
            P("mp", None),
            P(),
            P("dp"),
            rows,
            opt,
            opt,
            opt,
            opt,
        ),
        out_specs=(rows, rows, opt, opt, opt, opt, opt),
        check_vma=False,
    )
```

```python
import jax
import jax.numpy as jnp
from jax import lax
from jax.experimental import pallas as pl
from jax.experimental.pallas import tpu as pltpu
from jax.sharding import PartitionSpec as P

HDIM = 64
SLOT_TOKENS = 512
SHORT_TOKENS = 128
STEP = 3
NORM_EPS = 1e-12
BF = jnp.bfloat16
F32 = jnp.float32


def slot_masks(kind, sequence_lengths):
    pos = jnp.arange(SLOT_TOKENS, dtype=jnp.int32)
    block = pos // SHORT_TOKENS
    is_long = kind == 1
    segment = jnp.where(is_long, 0, block)
    inner = jnp.where(is_long, pos, pos % SHORT_TOKENS)
    picks = block[:, None] == jnp.arange(sequence_lengths.shape[0], dtype=jnp.int32)[None, :]
    short_len = jnp.sum(jnp.where(picks, sequence_lengths[None, :], 0), axis=1)
    seg_len = jnp.where(is_long, jnp.sum(sequence_lengths), short_len)
    valid = inner < seg_len
    allowed = (segment[:, None] == segment[None, :]) & valid[None, :]
    return (allowed, valid)


def dot(a, b):
    return lax.dot_general(a, b, (((1,), (0,)), ((), ())), preferred_element_type=F32)


def dot_t(a, b):
    return lax.dot_general(a, b, (((1,), (1,)), ((), ())), preferred_element_type=F32)


def t_dot(a, b):
    return lax.dot_general(a, b, (((0,), (0,)), ((), ())), preferred_element_type=F32)


def swap(value, axis, bit):
    size = lax.axis_size(axis)
    return lax.ppermute(value, axis, [(i, i ^ bit) for i in range(size)])


def both_cores(value):
    return (value, swap(value, "mp", 1))


def norm_parts(z):
    mean = jnp.mean(z, axis=-1, keepdims=True)
    centered = z - mean
    var = jnp.mean(centered * centered, axis=-1, keepdims=True)
    rstd = lax.rsqrt(var + NORM_EPS)
    return centered * rstd, rstd


def norm_back(dy, normed, rstd, gain):
    dn = dy * gain
    back = rstd * (
        dn
        - jnp.mean(dn, axis=-1, keepdims=True)
        - normed * jnp.mean(dn * normed, axis=-1, keepdims=True)
    )
    return back, jnp.sum(dy * normed, axis=0), jnp.sum(dy, axis=0), jnp.sum(back, axis=0)


VMEM = pl.BlockSpec(memory_space=pltpu.VMEM)
SMEM = pl.BlockSpec(memory_space=pltpu.SMEM)


def struct(shape, dtype):
    return jax.ShapeDtypeStruct(shape, dtype)


def key_codes(kind, lens, axis):
    shape = (SLOT_TOKENS, 1) if axis == 0 else (1, SLOT_TOKENS)
    pos = lax.broadcasted_iota(jnp.int32, shape, axis)
    block = pos >> 7
    short = jnp.where(
        block == 0, lens[0], jnp.where(block == 1, lens[1], jnp.where(block == 2, lens[2], lens[3]))
    )
    is_long = kind == 1
    inner = jnp.where(is_long, pos, pos & (SHORT_TOKENS - 1))
    length = jnp.where(is_long, lens[0] + lens[1] + lens[2] + lens[3], short)
    return jnp.where(inner < length, jnp.where(is_long, 0, block), -1)


def query_codes(kind, axis):
    shape = (SLOT_TOKENS, 1) if axis == 0 else (1, SLOT_TOKENS)
    pos = lax.broadcasted_iota(jnp.int32, shape, axis)
    return jnp.where(kind == 1, 0, pos >> 7)


def slot_info(info_ref):
    return info_ref[0], [info_ref[1 + i] for i in range(4)]


def forward_kernel(info, x, w, bias, wo, q_out, k_out, v_out, ctx_out, lse_out, part):
    kind, lens = slot_info(info)
    wide = ctx_out.shape[1]
    scale = HDIM ** (-0.5)
    xv = x[...]
    q_out[...] = ((dot_t(xv, w[:wide]) + bias[0:1]) * scale).astype(BF)
    k_out[...] = dot_t(xv, w[wide : 2 * wide]).astype(BF)
    v_out[...] = (dot_t(xv, w[2 * wide :]) + bias[1:2]).astype(BF)
    allowed = query_codes(kind, 0) == key_codes(kind, lens, 1)
    lower = lax.broadcasted_iota(jnp.int32, (1, 128), 1) < HDIM

    @pl.loop(0, wide // 128)
    def _(pair):
        at = pl.ds(pl.multiple_of(pair * 128, 128), 128)
        q, k, v = q_out[:, at], k_out[:, at], v_out[:, at]
        results = []
        for half in (lower, ~lower):
            s = dot_t(jnp.where(half, q, jnp.zeros_like(q)), k)
            s = jnp.where(allowed, s, -1000000000.0)
            top = jnp.max(s, axis=-1, keepdims=True)
            e = jnp.exp(s - top)
            total = jnp.sum(e, axis=-1, keepdims=True)
            results.append((dot(e.astype(BF), v) / total, top + jnp.log(total)))
        (ctx0, lse0), (ctx1, lse1) = results
        ctx_out[:, at] = jnp.where(lower, ctx0, ctx1).astype(BF)
        lse_out[:, at] = jnp.where(lower, lse0, lse1)

    part[...] = dot(ctx_out[...], wo[...]).astype(BF)


def backward_kernel(
    info, dz_two, own, other, normed, rstd, gain, q_in, k_in, v_in, ctx_in, lse_in, w, wo,
    dz_out, dzb_out, dq_out, dk_out, dv_out, sums, part, dctx,
):
    kind, lens = slot_info(info)
    wide = ctx_in.shape[1]
    scale = HDIM ** (-0.5)
    dx = dz_two[...] + (own[...].astype(F32) + other[...].astype(F32))
    unit = normed[...]
    dn = dx * gain[...]
    back = rstd[...] * (
        dn
        - jnp.mean(dn, axis=-1, keepdims=True)
        - unit * jnp.mean(dn * unit, axis=-1, keepdims=True)
    )
    dz_out[...] = back
    dzb_out[...] = back.astype(BF)
    sums[0:1] = jnp.sum(dx * unit, axis=0, keepdims=True)
    sums[1:2] = jnp.sum(dx, axis=0, keepdims=True)
    sums[2:3] = jnp.sum(back, axis=0, keepdims=True)
    sums[3:] = jnp.zeros((sums.shape[0] - 3, sums.shape[1]), F32)
    dctx[...] = dot_t(dzb_out[...], wo[...]).astype(BF)
    allowed = key_codes(kind, lens, 0) == query_codes(kind, 1)
    lower = lax.broadcasted_iota(jnp.int32, (1, 128), 1) < HDIM

    @pl.loop(0, wide // 128)
    def _(pair):
        at = pl.ds(pl.multiple_of(pair * 128, 128), 128)
        q, k, v, dc = q_in[:, at], k_in[:, at], v_in[:, at], dctx[:, at]
        lse_t = jnp.transpose(lse_in[:, at])
        prod_t = jnp.transpose(dc.astype(F32) * ctx_in[:, at].astype(F32))
        results = []
        for number, half in enumerate((lower, ~lower)):
            base = number * HDIM
            s = dot_t(k, jnp.where(half, q, jnp.zeros_like(q)))
            p = jnp.where(allowed, jnp.exp(s - lse_t[base : base + 1]), 0.0)
            dp = dot_t(v, jnp.where(half, dc, jnp.zeros_like(dc)))
            row = jnp.sum(prod_t[base : base + HDIM], axis=0, keepdims=True)
            ds = (p * (dp - row)).astype(BF)
            results.append((t_dot(ds, k), dot(ds, q), dot(p.astype(BF), dc)))
        for out, a, b in zip((dq_out, dk_out, dv_out), *results):
            out[:, at] = jnp.where(lower, a, b).astype(BF)

    part[...] = (
        dot(dq_out[...], w[:wide]) * scale
        + dot(dk_out[...], w[wide : 2 * wide])
        + dot(dv_out[...], w[2 * wide :])
    ).astype(BF)


def gradient_kernel(blocks, x, dq0, dq1, dk0, dk1, dv0, dv1, own, other, columns):
    scale = HDIM ** (-0.5)
    depth = own.shape[1]
    cols = own.shape[2]
    for piece, pair in enumerate(((dq0, dq1), (dk0, dk1), (dv0, dv1))):
        g = t_dot(x[:SLOT_TOKENS], pair[0][...]) + t_dot(x[SLOT_TOKENS:], pair[1][...])
        if piece == 0:
            g = g * scale
        mine, theirs = g[:, :cols], g[:, cols:]
        wide = g.shape[0]
        row = 0
        while row < wide:
            block, inside = divmod(piece * wide + row, depth)
            take = min(wide - row, depth - inside)
            own[block, inside : inside + take] = mine[row : row + take]
            other[block, inside : inside + take] = theirs[row : row + take].astype(BF)
            row += take
        total = jnp.sum(pair[0][...].astype(F32), axis=0, keepdims=True) + jnp.sum(
            pair[1][...].astype(F32), axis=0, keepdims=True
        )
        columns[piece : piece + 1] = total * (scale if piece == 0 else 1.0)
    columns[3:] = jnp.zeros((columns.shape[0] - 3, columns.shape[1]), F32)


def call(kernel, inputs, outputs, scratch=(), flops=0, name=None):
    size = sum(a.size * a.dtype.itemsize for a in list(inputs[0:]) + list(outputs))
    return pl.pallas_call(
        kernel,
        in_specs=[SMEM if a.ndim == 1 else VMEM for a in inputs],
        out_specs=[VMEM] * len(outputs),
        out_shape=list(outputs),
        scratch_shapes=list(scratch),
        cost_estimate=pl.CostEstimate(flops=flops, bytes_accessed=size, transcendentals=0),
        name=name,
    )(*inputs)


def scatter_sum(blocks, first, order):
    ndata = blocks.shape[0]
    rank = lax.axis_index("dp")
    cur = blocks[None]
    left = list(range(ndata.bit_length() - 1))
    for bit in order(left):
        low = sum(1 for b in left if b < bit)
        rest = cur.shape[2:]
        view = cur.reshape((cur.shape[1] >> (low + 1), 2, 1 << low) + rest)
        mine = (rank >> bit) & 1
        keep = lax.dynamic_index_in_dim(view, mine, 1, keepdims=False)
        send = lax.dynamic_index_in_dim(view, 1 - mine, 1, keepdims=False)
        got = swap(send.astype(BF), "dp", 1 << bit)
        cur = (keep.astype(F32) + got.astype(F32)).reshape((1, -1) + rest)
        left.remove(bit)
    return cur[0, 0]


def upward(left):
    return list(left)


def body(
    tokens,
    cotangent,
    qkv_weight,
    col_bias,
    out_weight,
    in_weight,
    in_bias,
    down_weight,
    vectors,
    slot_is_long,
    seq_len,
    master,
    first_moment,
    second_moment,
    average,
):
    rows = tokens.shape[0]
    scale = HDIM ** (-0.5)
    ndata = lax.axis_size("dp")
    nmodel = lax.axis_size("mp")
    core = lax.axis_index("mp") & 1
    pair = lax.axis_index("mp") >> 1
    vec = vectors.astype(F32)
    per_core = rows // 2 // SLOT_TOKENS

    cols = qkv_weight.shape[2]
    wide = 2 * cols
    wqkv = both_cores(jnp.transpose(qkv_weight, (0, 2, 1)))
    w_attn = jnp.concatenate(wqkv, axis=1).reshape(3 * wide, -1)
    bias = jnp.concatenate(both_cores(col_bias), axis=1).astype(F32)
    wo = jnp.concatenate(both_cores(out_weight), axis=0)
    w1 = both_cores(in_weight)
    b1 = both_cores(in_bias)
    w2 = both_cores(down_weight)
    model = tokens.shape[1]
    slot_flops = 2 * SLOT_TOKENS * model * wide

    x_mine = lax.dynamic_slice_in_dim(tokens, core * (rows // 2), rows // 2)
    cot_mine = lax.dynamic_slice_in_dim(cotangent, core * (rows // 2), rows // 2)
    kinds = lax.dynamic_slice_in_dim(slot_is_long, core * per_core, per_core)
    lengths = lax.dynamic_slice_in_dim(seq_len, core * per_core, per_core)
    n = range(per_core)
    info = [jnp.concatenate([kinds[i : i + 1], lengths[i]]) for i in n]
    x = [x_mine[i * SLOT_TOKENS : (i + 1) * SLOT_TOKENS] for i in n]
    cot = [cot_mine[i * SLOT_TOKENS : (i + 1) * SLOT_TOKENS] for i in n]
    masks = [slot_masks(kinds[i], lengths[i]) for i in n]

    def phase_one(i):
        act = struct((SLOT_TOKENS, wide), BF)
        *kept, part = call(
            forward_kernel,
            (info[i], x[i], w_attn, bias, wo),
            (act, act, act, act, struct((SLOT_TOKENS, wide), F32), struct((SLOT_TOKENS, model), BF)),
            flops=6 * slot_flops,
            name="attn_fwd",
        )
        return kept, part

    def total(part, other):
        return part.astype(F32) + other.astype(F32)

    def phase_two(i, part, other):
        z = x[i].astype(F32) + total(part, other) + vec[4]
        normed, rstd = norm_parts(z)
        x_one = normed * vec[0] + vec[1]
        xb = x_one.astype(BF)
        hidden, slope, out = [], [], 0.0
        for g in range(2):
            pre = dot(xb, w1[g]) + b1[g].astype(F32)
            phi = 0.5 * (1.0 + lax.erf(pre * 2.0 ** (-0.5)))
            hidden.append((pre * phi).astype(BF))
            bell = jnp.exp(-0.5 * pre * pre) * 0.3989422804014327
            slope.append((phi + pre * bell).astype(BF))
            out = out + dot(hidden[g], w2[g])
        return (normed, rstd, x_one, xb, hidden, slope), out.astype(BF)

    def phase_three(i, saved, part, other):
        normed, rstd, x_one, xb, hidden, slope = saved
        z = x_one + total(part, other) + vec[5]
        n2, r2 = norm_parts(z)
        out = (n2 * vec[2] + vec[3]).astype(BF)
        dy = cot[i].astype(F32) * masks[i][1][:, None].astype(F32)
        dz, dg, dbeta, db = norm_back(dy, n2, r2, vec[2])
        dzb = dz.astype(BF)
        dpre, back = [], 0.0
        for g in range(2):
            dpre.append((dot_t(dzb, w2[g]) * slope[g].astype(F32)).astype(BF))
            back = back + dot_t(dpre[g], w1[g])
        return out, (dz, dzb, dpre, (dg, dbeta, db)), back.astype(BF)

    def phase_four(i, first, second, third, part, other):
        q, k, v, ctx, lse = first
        normed, rstd = second[:2]
        act = struct((SLOT_TOKENS, wide), BF)
        dz, dzb, dq, dk, dv, sums, back = call(
            backward_kernel,
            (info[i], third[0], part, other, normed, rstd, vec[0:1], q, k, v, ctx, lse, w_attn, wo),
            (
                struct((SLOT_TOKENS, model), F32),
                struct((SLOT_TOKENS, model), BF),
                act,
                act,
                act,
                struct((8, model), F32),
                struct((SLOT_TOKENS, model), BF),
            ),
            scratch=(pltpu.VMEM((SLOT_TOKENS, wide), BF),),
            flops=10 * slot_flops,
            name="attn_bwd",
        )
        return (dz, dzb, (dq, dk, dv), (sums[0], sums[1], sums[2])), back

    across = lambda part: swap(part, "mp", 2)
    one = [phase_one(i) for i in n]
    one_r = [across(one[i][1]) for i in n]
    two = [phase_two(i, one[i][1], one_r[i]) for i in n]
    two_r = [across(two[i][1]) for i in n]
    three = [phase_three(i, two[i][0], two[i][1], two_r[i]) for i in n]
    three_r = [across(three[i][2]) for i in n]
    four = [phase_four(i, one[i][0], two[i][0], three[i][1], three[i][2], three_r[i]) for i in n]
    four_r = [across(four[i][1]) for i in n]

    def whole(half, other):
        first = jnp.where(core == 0, half, other)
        second = jnp.where(core == 0, other, half)
        return jnp.concatenate([first, second])

    out_half = jnp.concatenate([three[i][0] for i in n])
    output = whole(out_half, swap(out_half, "mp", 1))
    gi_half = jnp.concatenate([four[i][0][0] + total(four[i][1], four_r[i]) for i in n])
    grad_input = whole(gi_half, swap(gi_half, "mp", 1))

    def over_cores(parts):
        return parts[0] + swap(parts[1].astype(BF), "mp", 1).astype(F32)

    cat = lambda f: jnp.concatenate([f(i) for i in n])
    xb_all = cat(lambda i: two[i][0][3])
    dz2_all = cat(lambda i: three[i][1][1])
    g_down, g_in, g_inb = [], [], []
    for g in range(2):
        dpre = cat(lambda i: three[i][1][2][g])
        g_down.append(t_dot(cat(lambda i: two[i][0][4][g]), dz2_all))
        g_in.append(t_dot(xb_all, dpre))
        g_inb.append(jnp.sum(dpre.astype(F32), axis=0))
    s_down = scatter_sum(over_cores(g_down).reshape(ndata, -1, g_down[0].shape[1]), None, upward)
    s_in = scatter_sum(over_cores(g_in).reshape(ndata, -1, g_in[0].shape[1]), None, upward)

    ctx_all = cat(lambda i: one[i][0][3])
    dz1_all = cat(lambda i: four[i][0][1])
    g_full = t_dot(ctx_all, dz1_all)
    g_out = [g_full[:cols], g_full[cols:]]
    s_out = scatter_sum(over_cores(g_out).reshape(ndata, -1, model), None, upward)
    pairs = [four[i][0][2][t] for t in range(3) for i in n]
    block = (ndata, 3 * model // ndata, cols)
    g_own, g_other, g_sums = call(
        lambda *refs: gradient_kernel(ndata, *refs),
        (x_mine, *pairs),
        (struct(block, F32), struct(block, BF), struct((8, wide), F32)),
        flops=6 * slot_flops,
        name="attn_grad",
    )
    s_qkv = scatter_sum(g_own + swap(g_other, "mp", 1).astype(F32), None, upward)
    g_col = [jnp.stack([g_sums[0, c], g_sums[2, c]]) for c in (slice(0, cols), slice(cols, wide))]

    add = lambda t: sum(t[1:], t[0])
    g1, be1, bo = (add([four[i][0][3][t] for i in n]) for t in range(3))
    g2, be2, b2 = (add([three[i][1][3][t] for i in n]) for t in range(3))
    g_vec = jnp.stack([g1, be1, g2, be2, bo, b2]).reshape(nmodel, -1)
    small = []
    for g in range(2):
        owner = 2 * pair + (core if g == 0 else 1 - core)
        share = lax.dynamic_index_in_dim(g_vec, owner, 0, keepdims=False)
        small.append(
            jnp.concatenate([g_col[g].reshape(ndata, -1), g_inb[g].reshape(ndata, -1), share.reshape(ndata, -1)], axis=1)
        )
    s_small = scatter_sum(over_cores(small), None, upward)
    n_vec = g_vec.shape[1] // ndata

    grad = jnp.concatenate([s_qkv.reshape(-1), s_out.reshape(-1), s_in.reshape(-1), s_down.reshape(-1), s_small])
    grad = (grad / ndata).reshape(master.shape)
    vector_grad = (s_small[-n_vec:] / ndata).reshape(1, 1, -1)
    new_first = 0.5 * first_moment + 0.5 * grad
    new_second = 0.5 * second_moment + 0.5 * grad * grad
    corr = 1.0 - 0.5**STEP
    new_master = master - 0.02 * (
        new_first / corr / (jnp.sqrt(new_second / corr) + 1e-08) + 0.01 * master
    )
    new_average = 0.75 * average + 0.25 * new_master
    return (output, grad_input, vector_grad, new_master, new_first, new_second, new_average)


def solution(mesh):
    rows = P("dp", None)
    opt = P("mp", "dp", None)
    return jax.shard_map(
        body,
        mesh=mesh,
        in_specs=(
            rows,
            rows,
            P(None, None, "mp"),
            P(None, "mp"),
            P("mp", None),
            P(None, "mp"),
            P("mp"),
            P("mp", None),
            P(),
            P("dp"),
            rows,
            opt,
            opt,
            opt,
            opt,
        ),
        out_specs=(rows, rows, opt, opt, opt, opt, opt),
        check_vma=False,
    )
```

```python
import jax
import jax.numpy as jnp
from jax import lax
from jax.experimental import pallas as pl
from jax.experimental.pallas import tpu as pltpu
from jax.sharding import PartitionSpec as P

HDIM = 64
SLOT_TOKENS = 512
SHORT_TOKENS = 128
STEP = 3
NORM_EPS = 1e-12
BF = jnp.bfloat16
F32 = jnp.float32


def slot_masks(kind, sequence_lengths):
    pos = jnp.arange(SLOT_TOKENS, dtype=jnp.int32)
    block = pos // SHORT_TOKENS
    is_long = kind == 1
    segment = jnp.where(is_long, 0, block)
    inner = jnp.where(is_long, pos, pos % SHORT_TOKENS)
    picks = block[:, None] == jnp.arange(sequence_lengths.shape[0], dtype=jnp.int32)[None, :]
    short_len = jnp.sum(jnp.where(picks, sequence_lengths[None, :], 0), axis=1)
    seg_len = jnp.where(is_long, jnp.sum(sequence_lengths), short_len)
    valid = inner < seg_len
    allowed = (segment[:, None] == segment[None, :]) & valid[None, :]
    return (allowed, valid)


def dot(a, b):
    return lax.dot_general(a, b, (((1,), (0,)), ((), ())), preferred_element_type=F32)


def dot_t(a, b):
    return lax.dot_general(a, b, (((1,), (1,)), ((), ())), preferred_element_type=F32)


def t_dot(a, b):
    return lax.dot_general(a, b, (((0,), (0,)), ((), ())), preferred_element_type=F32)


def swap(value, axis, bit):
    size = lax.axis_size(axis)
    return lax.ppermute(value, axis, [(i, i ^ bit) for i in range(size)])


def both_cores(value):
    return (value, swap(value, "mp", 1))


def norm_parts(z):
    mean = jnp.mean(z, axis=-1, keepdims=True)
    centered = z - mean
    var = jnp.mean(centered * centered, axis=-1, keepdims=True)
    rstd = lax.rsqrt(var + NORM_EPS)
    return centered * rstd, rstd


def norm_back(dy, normed, rstd, gain):
    dn = dy * gain
    back = rstd * (
        dn
        - jnp.mean(dn, axis=-1, keepdims=True)
        - normed * jnp.mean(dn * normed, axis=-1, keepdims=True)
    )
    return back, jnp.sum(dy * normed, axis=0), jnp.sum(dy, axis=0), jnp.sum(back, axis=0)


VMEM = pl.BlockSpec(memory_space=pltpu.VMEM)
SMEM = pl.BlockSpec(memory_space=pltpu.SMEM)


def struct(shape, dtype):
    return jax.ShapeDtypeStruct(shape, dtype)


def key_codes(kind, lens, axis):
    shape = (SLOT_TOKENS, 1) if axis == 0 else (1, SLOT_TOKENS)
    pos = lax.broadcasted_iota(jnp.int32, shape, axis)
    block = pos >> 7
    short = jnp.where(
        block == 0, lens[0], jnp.where(block == 1, lens[1], jnp.where(block == 2, lens[2], lens[3]))
    )
    is_long = kind == 1
    inner = jnp.where(is_long, pos, pos & (SHORT_TOKENS - 1))
    length = jnp.where(is_long, lens[0] + lens[1] + lens[2] + lens[3], short)
    return jnp.where(inner < length, jnp.where(is_long, 0, block), -1)


def query_codes(kind, axis):
    shape = (SLOT_TOKENS, 1) if axis == 0 else (1, SLOT_TOKENS)
    pos = lax.broadcasted_iota(jnp.int32, shape, axis)
    return jnp.where(kind == 1, 0, pos >> 7)


def slot_info(info_ref):
    return info_ref[0], [info_ref[1 + i] for i in range(4)]


def forward_kernel(info, x, w, bias, wo, q_out, k_out, v_out, ctx_out, lse_out, part):
    kind, lens = slot_info(info)
    wide = ctx_out.shape[1]
    scale = HDIM ** (-0.5)
    xv = x[...]
    q_out[...] = ((dot_t(xv, w[:wide]) + bias[0:1]) * scale).astype(BF)
    k_out[...] = dot_t(xv, w[wide : 2 * wide]).astype(BF)
    v_out[...] = (dot_t(xv, w[2 * wide :]) + bias[1:2]).astype(BF)
    allowed = query_codes(kind, 0) == key_codes(kind, lens, 1)
    lower = lax.broadcasted_iota(jnp.int32, (1, 128), 1) < HDIM

    @pl.loop(0, wide // 128)
    def _(pair):
        at = pl.ds(pl.multiple_of(pair * 128, 128), 128)
        q, k, v = q_out[:, at], k_out[:, at], v_out[:, at]
        results = []
        for half in (lower, ~lower):
            s = dot_t(jnp.where(half, q, jnp.zeros_like(q)), k)
            s = jnp.where(allowed, s, -1000000000.0)
            top = jnp.max(s, axis=-1, keepdims=True)
            e = jnp.exp(s - top)
            total = jnp.sum(e, axis=-1, keepdims=True)
            results.append((dot(e.astype(BF), v) / total, top + jnp.log(total)))
        (ctx0, lse0), (ctx1, lse1) = results
        ctx_out[:, at] = jnp.where(lower, ctx0, ctx1).astype(BF)
        lse_out[:, at] = jnp.where(lower, lse0, lse1)

    part[...] = dot(ctx_out[...], wo[...]).astype(BF)


def backward_kernel(
    info, dz_two, own, other, normed, rstd, gain, q_in, k_in, v_in, ctx_in, lse_in, w, wo,
    dz_out, dzb_out, dq_out, dk_out, dv_out, sums, part, dctx,
):
    kind, lens = slot_info(info)
    wide = ctx_in.shape[1]
    scale = HDIM ** (-0.5)
    dx = dz_two[...] + (own[...].astype(F32) + other[...].astype(F32))
    unit = normed[...]
    dn = dx * gain[...]
    back = rstd[...] * (
        dn
        - jnp.mean(dn, axis=-1, keepdims=True)
        - unit * jnp.mean(dn * unit, axis=-1, keepdims=True)
    )
    dz_out[...] = back
    dzb_out[...] = back.astype(BF)
    sums[0:1] = jnp.sum(dx * unit, axis=0, keepdims=True)
    sums[1:2] = jnp.sum(dx, axis=0, keepdims=True)
    sums[2:3] = jnp.sum(back, axis=0, keepdims=True)
    sums[3:] = jnp.zeros((sums.shape[0] - 3, sums.shape[1]), F32)
    dctx[...] = dot_t(dzb_out[...], wo[...]).astype(BF)
    allowed = key_codes(kind, lens, 0) == query_codes(kind, 1)
    lower = lax.broadcasted_iota(jnp.int32, (1, 128), 1) < HDIM

    @pl.loop(0, wide // 128)
    def _(pair):
        at = pl.ds(pl.multiple_of(pair * 128, 128), 128)
        q, k, v, dc = q_in[:, at], k_in[:, at], v_in[:, at], dctx[:, at]
        lse_t = jnp.transpose(lse_in[:, at])
        prod_t = jnp.transpose(dc.astype(F32) * ctx_in[:, at].astype(F32))
        results = []
        for number, half in enumerate((lower, ~lower)):
            base = number * HDIM
            s = dot_t(k, jnp.where(half, q, jnp.zeros_like(q)))
            p = jnp.where(allowed, jnp.exp(s - lse_t[base : base + 1]), 0.0)
            dp = dot_t(v, jnp.where(half, dc, jnp.zeros_like(dc)))
            row = jnp.sum(prod_t[base : base + HDIM], axis=0, keepdims=True)
            ds = (p * (dp - row)).astype(BF)
            results.append((t_dot(ds, k), dot(ds, q), dot(p.astype(BF), dc)))
        for out, a, b in zip((dq_out, dk_out, dv_out), *results):
            out[:, at] = jnp.where(lower, a, b).astype(BF)

    part[...] = (
        dot(dq_out[...], w[:wide]) * scale
        + dot(dk_out[...], w[wide : 2 * wide])
        + dot(dv_out[...], w[2 * wide :])
    ).astype(BF)


def gradient_kernel(blocks, x, dq0, dq1, dk0, dk1, dv0, dv1, own, other, columns):
    scale = HDIM ** (-0.5)
    depth = own.shape[1]
    cols = own.shape[2]
    for piece, pair in enumerate(((dq0, dq1), (dk0, dk1), (dv0, dv1))):
        g = t_dot(x[:SLOT_TOKENS], pair[0][...]) + t_dot(x[SLOT_TOKENS:], pair[1][...])
        if piece == 0:
            g = g * scale
        mine, theirs = g[:, :cols], g[:, cols:]
        wide = g.shape[0]
        row = 0
        while row < wide:
            block, inside = divmod(piece * wide + row, depth)
            take = min(wide - row, depth - inside)
            own[block, inside : inside + take] = mine[row : row + take]
            other[block, inside : inside + take] = theirs[row : row + take].astype(BF)
            row += take
        total = jnp.sum(pair[0][...].astype(F32), axis=0, keepdims=True) + jnp.sum(
            pair[1][...].astype(F32), axis=0, keepdims=True
        )
        columns[piece : piece + 1] = total * (scale if piece == 0 else 1.0)
    columns[3:] = jnp.zeros((columns.shape[0] - 3, columns.shape[1]), F32)


def call(kernel, inputs, outputs, scratch=(), flops=0, name=None):
    size = sum(a.size * a.dtype.itemsize for a in list(inputs[0:]) + list(outputs))
    return pl.pallas_call(
        kernel,
        in_specs=[SMEM if a.ndim == 1 else VMEM for a in inputs],
        out_specs=[VMEM] * len(outputs),
        out_shape=list(outputs),
        scratch_shapes=list(scratch),
        cost_estimate=pl.CostEstimate(flops=flops, bytes_accessed=size, transcendentals=0),
        name=name,
    )(*inputs)


def scatter_step(cur, bit):
    mine = (lax.axis_index("dp") >> bit) & 1
    view = cur.reshape((-1, 2) + cur.shape[1:])
    keep = lax.dynamic_index_in_dim(view, mine, 1, keepdims=False)
    send = lax.dynamic_index_in_dim(view, 1 - mine, 1, keepdims=False)
    return keep.astype(F32) + swap(send.astype(BF), "dp", 1 << bit).astype(F32)


def scatter_sum(blocks, first=0):
    for bit in range(first, lax.axis_size("dp").bit_length() - 1):
        blocks = scatter_step(blocks, bit)
    return blocks[0]


def body(
    tokens,
    cotangent,
    qkv_weight,
    col_bias,
    out_weight,
    in_weight,
    in_bias,
    down_weight,
    vectors,
    slot_is_long,
    seq_len,
    master,
    first_moment,
    second_moment,
    average,
):
    rows = tokens.shape[0]
    scale = HDIM ** (-0.5)
    ndata = lax.axis_size("dp")
    nmodel = lax.axis_size("mp")
    core = lax.axis_index("mp") & 1
    pair = lax.axis_index("mp") >> 1
    vec = vectors.astype(F32)
    per_core = rows // 2 // SLOT_TOKENS

    cols = qkv_weight.shape[2]
    wide = 2 * cols
    wqkv = both_cores(jnp.transpose(qkv_weight, (0, 2, 1)))
    w_attn = jnp.concatenate(wqkv, axis=1).reshape(3 * wide, -1)
    bias = jnp.concatenate(both_cores(col_bias), axis=1).astype(F32)
    wo = jnp.concatenate(both_cores(out_weight), axis=0)
    w1 = both_cores(in_weight)
    b1 = both_cores(in_bias)
    w2 = both_cores(down_weight)
    model = tokens.shape[1]
    slot_flops = 2 * SLOT_TOKENS * model * wide

    x_mine = lax.dynamic_slice_in_dim(tokens, core * (rows // 2), rows // 2)
    cot_mine = lax.dynamic_slice_in_dim(cotangent, core * (rows // 2), rows // 2)
    kinds = lax.dynamic_slice_in_dim(slot_is_long, core * per_core, per_core)
    lengths = lax.dynamic_slice_in_dim(seq_len, core * per_core, per_core)
    n = range(per_core)
    info = [jnp.concatenate([kinds[i : i + 1], lengths[i]]) for i in n]
    x = [x_mine[i * SLOT_TOKENS : (i + 1) * SLOT_TOKENS] for i in n]
    cot = [cot_mine[i * SLOT_TOKENS : (i + 1) * SLOT_TOKENS] for i in n]
    masks = [slot_masks(kinds[i], lengths[i]) for i in n]

    def phase_one(i):
        act = struct((SLOT_TOKENS, wide), BF)
        *kept, part = call(
            forward_kernel,
            (info[i], x[i], w_attn, bias, wo),
            (act, act, act, act, struct((SLOT_TOKENS, wide), F32), struct((SLOT_TOKENS, model), BF)),
            flops=6 * slot_flops,
            name="attn_fwd",
        )
        return kept, part

    def total(part, other):
        return part.astype(F32) + other.astype(F32)

    def phase_two(i, part, other):
        z = x[i].astype(F32) + total(part, other) + vec[4]
        normed, rstd = norm_parts(z)
        x_one = normed * vec[0] + vec[1]
        xb = x_one.astype(BF)
        hidden, slope, out = [], [], 0.0
        for g in range(2):
            pre = dot(xb, w1[g]) + b1[g].astype(F32)
            phi = 0.5 * (1.0 + lax.erf(pre * 2.0 ** (-0.5)))
            hidden.append((pre * phi).astype(BF))
            bell = jnp.exp(-0.5 * pre * pre) * 0.3989422804014327
            slope.append((phi + pre * bell).astype(BF))
            out = out + dot(hidden[g], w2[g])
        return (normed, rstd, x_one, xb, hidden, slope), out.astype(BF)

    def phase_three(i, saved, part, other):
        normed, rstd, x_one, xb, hidden, slope = saved
        z = x_one + total(part, other) + vec[5]
        n2, r2 = norm_parts(z)
        out = (n2 * vec[2] + vec[3]).astype(BF)
        dy = cot[i].astype(F32) * masks[i][1][:, None].astype(F32)
        dz, dg, dbeta, db = norm_back(dy, n2, r2, vec[2])
        dzb = dz.astype(BF)
        dpre, back = [], 0.0
        for g in range(2):
            dpre.append((dot_t(dzb, w2[g]) * slope[g].astype(F32)).astype(BF))
            back = back + dot_t(dpre[g], w1[g])
        return out, (dz, dzb, dpre, (dg, dbeta, db)), back.astype(BF)

    def phase_four(i, first, second, third, part, other):
        q, k, v, ctx, lse = first
        normed, rstd = second[:2]
        act = struct((SLOT_TOKENS, wide), BF)
        dz, dzb, dq, dk, dv, sums, back = call(
            backward_kernel,
            (info[i], third, part, other, normed, rstd, vec[0:1], q, k, v, ctx, lse, w_attn, wo),
            (
                struct((SLOT_TOKENS, model), F32),
                struct((SLOT_TOKENS, model), BF),
                act,
                act,
                act,
                struct((8, model), F32),
                struct((SLOT_TOKENS, model), BF),
            ),
            scratch=(pltpu.VMEM((SLOT_TOKENS, wide), BF),),
            flops=10 * slot_flops,
            name="attn_bwd",
        )
        return (dz, dzb, (dq, dk, dv), (sums[0], sums[1], sums[2])), back

    across = lambda part: swap(part, "mp", 2)
    one = [phase_one(i) for i in n]
    one_r = [across(one[i][1]) for i in n]
    two = [phase_two(i, one[i][1], one_r[i]) for i in n]
    two_r = [across(two[i][1]) for i in n]
    three = [phase_three(i, two[i][0], two[i][1], two_r[i]) for i in n]
    three_r = [across(three[i][2]) for i in n]
    def over_cores(parts):
        return parts[0] + swap(parts[1].astype(BF), "mp", 1).astype(F32)

    cat = lambda f: jnp.concatenate([f(i) for i in n])
    xb_all = cat(lambda i: two[i][0][3])
    dz2_all = cat(lambda i: three[i][1][1])
    g_down, g_in, g_inb = [], [], []
    for g in range(2):
        dpre = cat(lambda i: three[i][1][2][g])
        g_down.append(t_dot(cat(lambda i: two[i][0][4][g]), dz2_all))
        g_in.append(t_dot(xb_all, dpre))
        g_inb.append(jnp.sum(dpre.astype(F32), axis=0))
    ffn = [over_cores(g).reshape(ndata, -1, model) for g in (g_in, g_down)]
    dz_two = [three[i][1][0] for i in n]
    dz_two[0], *ffn = lax.optimization_barrier((dz_two[0], *ffn))
    ffn = [scatter_step(t, 0) for t in ffn]

    four = [phase_four(i, one[i][0], two[i][0], dz_two[i], three[i][2], three_r[i]) for i in n]
    four_r = [across(four[i][1]) for i in n]

    def whole(half, other):
        first = jnp.where(core == 0, half, other)
        second = jnp.where(core == 0, other, half)
        return jnp.concatenate([first, second])

    out_half = jnp.concatenate([three[i][0] for i in n])
    output = whole(out_half, swap(out_half, "mp", 1))
    gi_half = jnp.concatenate([four[i][0][0] + total(four[i][1], four_r[i]) for i in n])
    grad_input = whole(gi_half, swap(gi_half, "mp", 1))

    ctx_all = cat(lambda i: one[i][0][3])
    dz1_all = cat(lambda i: four[i][0][1])
    g_full = t_dot(ctx_all, dz1_all)
    g_out = [g_full[:cols], g_full[cols:]]
    s_out = scatter_sum(over_cores(g_out).reshape(ndata, -1, model))
    pairs = [four[i][0][2][t] for t in range(3) for i in n]
    pairs[0], *ffn = lax.optimization_barrier((pairs[0], *ffn))
    s_in, s_down = (scatter_sum(t, 1) for t in ffn)
    block = (ndata, 3 * model // ndata, cols)
    g_own, g_other, g_sums = call(
        lambda *refs: gradient_kernel(ndata, *refs),
        (x_mine, *pairs),
        (struct(block, F32), struct(block, BF), struct((8, wide), F32)),
        flops=6 * slot_flops,
        name="attn_grad",
    )
    s_qkv = scatter_sum(g_own + swap(g_other, "mp", 1).astype(F32))
    g_col = [jnp.stack([g_sums[0, c], g_sums[2, c]]) for c in (slice(0, cols), slice(cols, wide))]

    add = lambda t: sum(t[1:], t[0])
    g1, be1, bo = (add([four[i][0][3][t] for i in n]) for t in range(3))
    g2, be2, b2 = (add([three[i][1][3][t] for i in n]) for t in range(3))
    g_vec = jnp.stack([g1, be1, g2, be2, bo, b2]).reshape(nmodel, -1)
    small = []
    for g in range(2):
        owner = 2 * pair + (core if g == 0 else 1 - core)
        share = lax.dynamic_index_in_dim(g_vec, owner, 0, keepdims=False)
        small.append(
            jnp.concatenate([g_col[g].reshape(ndata, -1), g_inb[g].reshape(ndata, -1), share.reshape(ndata, -1)], axis=1)
        )
    s_small = scatter_sum(over_cores(small))
    n_vec = g_vec.shape[1] // ndata

    grad = jnp.concatenate([s_qkv.reshape(-1), s_out.reshape(-1), s_in.reshape(-1), s_down.reshape(-1), s_small])
    grad = (grad / ndata).reshape(master.shape)
    vector_grad = (s_small[-n_vec:] / ndata).reshape(1, 1, -1)
    new_first = 0.5 * first_moment + 0.5 * grad
    new_second = 0.5 * second_moment + 0.5 * grad * grad
    corr = 1.0 - 0.5**STEP
    new_master = master - 0.02 * (
        new_first / corr / (jnp.sqrt(new_second / corr) + 1e-08) + 0.01 * master
    )
    new_average = 0.75 * average + 0.25 * new_master
    return (output, grad_input, vector_grad, new_master, new_first, new_second, new_average)


def solution(mesh):
    rows = P("dp", None)
    opt = P("mp", "dp", None)
    return jax.shard_map(
        body,
        mesh=mesh,
        in_specs=(
            rows,
            rows,
            P(None, None, "mp"),
            P(None, "mp"),
            P("mp", None),
            P(None, "mp"),
            P("mp"),
            P("mp", None),
            P(),
            P("dp"),
            rows,
            opt,
            opt,
            opt,
            opt,
        ),
        out_specs=(rows, rows, opt, opt, opt, opt, opt),
        check_vma=False,
    )
```
